32 devices in a mesh: groups: 1, rank: 32 (over z, y, x, core).
Axes of the slice: x: 2, y: 2, z: 4, core: 2. Of those that a mesh axis runs over, the one named last changes fastest.
Arguments:
- core: float32 [256, 256, 256], P('rank', 'groups'), may hold values from -6 to 6
- x_factor: float32 [1536, 256], P('groups'), may hold values from -0.375 to 0.375
- y_factor: float32 [2048, 256], P('groups'), may hold values from -0.375 to 0.375
- z_factor: float32 [256, 1536], P('rank', 'groups'), may hold values from -0.375 to 0.375
- offsets: int32 [8], P('groups'), may hold values from 0 to 1535, as said below
- initial: float32 [1536, 8, 2048], P('rank', 'groups'), may hold values from -80 to 80
Outputs:
- max_error: float32 [1], P('groups')
- psnr: float32 [8], P('groups')
- ssim_five: float32 [1536, 8, 2048], P('rank', 'groups')
- ssim_seven: float32 [1536, 8, 2048], P('rank', 'groups')
- ssim_eleven: float32 [1536, 8, 2048], P('rank', 'groups')
The draws below stay inside these ranges and needn't reach their ends.
Inputs may be any that keep to these rules, and one draw needn't show every extreme that they name: `offsets`: 8 distinct planes in increasing order.
All inputs are finite; a program needn't handle non-finite values.
Results may differ from the reference program's by a relative error of at most 0.000075.
Values sent between devices are 32-bit elements; how exact they have to be, the bound alone decides.
A program may use at most 128 MiB of HBM per device.

```python
import jax
import jax.numpy as jnp
from jax import lax

R = 256
NX = 1536
NY = 2048
NZ = 1536
PLANES = 8


def draw_initial(key, part):
    keys = jax.random.split(jax.random.fold_in(key, 11), 3)
    positions = jnp.arange(NX, dtype=jnp.float32) / float(NX)
    base = jnp.clip(jax.random.normal(keys[0], (NX, PLANES, NY), jnp.float32), -5.0, 5.0)
    rising = jnp.exp(positions * jnp.log(4.0))
    row_scale = rising * jnp.exp(jax.random.uniform(keys[1], (NX,), jnp.float32, -0.35, 0.35))
    column_scale = jnp.exp(jax.random.uniform(keys[2], (NY,), jnp.float32, -0.7, 0.7))
    return base * row_scale[:, None, None] * column_scale[None, None, :]


def draw_offsets(key, part):
    shuffled = jax.random.permutation(jax.random.fold_in(key, 23), NZ)
    return jnp.sort(shuffled[:PLANES]).astype(jnp.int32)


def steps_of(key, dims, pieces, low, top_value):
    gain, own = 1.0, jax.random.fold_in(key, 6)
    for dim, shards_of in pieces:
        heights = jnp.exp(jax.random.uniform(jax.random.fold_in(own, dim), (shards_of,), jnp.float32, low / len(pieces), top_value / len(pieces)))
        gain = gain * jnp.repeat(heights, dims[dim] // shards_of).reshape([-1 if axis == dim else 1 for axis in range(len(dims))])
    return gain


def noise(own_key, dims, scale, reach, pieces=(), kind=jnp.bfloat16):
    values = scale * jax.random.normal(own_key, dims, jnp.float32)
    if pieces:
        values = values * steps_of(own_key, dims, pieces, -0.22, 0.18)
    return jnp.clip(values, -reach, reach).astype(kind)


def setup_inputs(seed: int = 0, part: int = 0) -> dict:
    key_of = jax.random.split(jax.random.key(seed), 7)
    own_keys = jax.random.split(jax.random.fold_in(key_of[6], part), 7)
    return {
        "core": noise(own_keys[0], (R, R, R), 1.0, 6.0, ((0, 32),), jnp.float32),
        "x_factor": noise(own_keys[1], (NX, R), R ** -0.5, 0.375, (), jnp.float32),
        "y_factor": noise(own_keys[2], (NY, R), R ** -0.5, 0.375, (), jnp.float32),
        "z_factor": noise(own_keys[3], (R, NZ), R ** -0.5, 0.375, ((0, 32),), jnp.float32),
        "offsets": draw_offsets(jax.random.fold_in(jax.random.fold_in(key_of[6], part), 71), part),
        "initial": draw_initial(jax.random.fold_in(jax.random.fold_in(key_of[6], part), 71), part),
    }


peak_value = 64.0
first_const = (0.01 * peak_value) * (0.01 * peak_value)
second_const = (0.03 * peak_value) * (0.03 * peak_value)
epsilon = 1e-6


def box_sums(values, window):
    margin = window // 2
    length = values.shape[0]
    across = values.shape[1]
    padded = jnp.pad(values, ((margin, margin), (0, 0)))
    row_sums = padded[0:length]
    for step_index in range(1, window):
        row_sums = row_sums + padded[step_index:step_index + length]
    padded = jnp.pad(row_sums, ((0, 0), (margin, margin)))
    summed = padded[:, 0:across]
    for step_index in range(1, window):
        summed = summed + padded[:, step_index:step_index + across]
    return summed


def similarity(sum_target, sum_rebuilt, sum_tt, sum_rr, sum_tr, window):
    window_area = float(window * window)
    mean_target = sum_target / window_area
    mean_rebuilt = sum_rebuilt / window_area
    var_target = sum_tt / window_area - mean_target * mean_target
    var_rebuilt = sum_rr / window_area - mean_rebuilt * mean_rebuilt
    covar = sum_tr / window_area - mean_target * mean_rebuilt
    upper = (2.0 * mean_target * mean_rebuilt + first_const) * (2.0 * covar + second_const)
    lower = (mean_target * mean_target + mean_rebuilt * mean_rebuilt + first_const) * (var_target + var_rebuilt + second_const)
    return upper / lower


def plane_maps(pair):
    target_plane, rebuilt_plane = pair
    results = []
    for window in (5, 7, 11):
        results.append(similarity(box_sums(target_plane, window), box_sums(rebuilt_plane, window),
                                  box_sums(target_plane * target_plane, window),
                                  box_sums(rebuilt_plane * rebuilt_plane, window),
                                  box_sums(target_plane * rebuilt_plane, window), window))
    return results[0], results[1], results[2]


def reference(core, x_factor, y_factor, z_factor, offsets, initial):
    exact = lax.Precision.HIGHEST
    picked = jnp.take(z_factor, offsets.astype(jnp.int32), axis=1)
    planes_core = jnp.einsum("kab,kp->pab", core, picked, precision=exact)
    along_y = jnp.einsum("pab,yb->pay", planes_core, y_factor, precision=exact)
    rebuilt = jnp.einsum("xa,pay->xpy", x_factor, along_y, precision=exact)
    misfit = initial - rebuilt
    max_error = jnp.max(jnp.abs(misfit)).reshape(1)
    mean_square = jnp.sum(misfit * misfit, axis=(0, 2)) / float(NX * NY)
    psnr = 10.0 * jnp.log10(peak_value * peak_value / (mean_square + epsilon))
    maps = lax.map(plane_maps, (jnp.moveaxis(initial, 1, 0), jnp.moveaxis(rebuilt, 1, 0)))
    return (max_error, psnr, jnp.moveaxis(maps[0], 0, 1), jnp.moveaxis(maps[1], 0, 1),
            jnp.moveaxis(maps[2], 0, 1))
```

```python
import functools

import jax
import jax.numpy as jnp
from jax import lax
from jax.experimental import pallas as pl
from jax.experimental.pallas import tpu as pltpu
from jax.sharding import PartitionSpec as P

peak_value = 64.0
first_const = 0.01 * peak_value * (0.01 * peak_value)
second_const = 0.03 * peak_value * (0.03 * peak_value)
epsilon = 1e-06
windows = (5, 7, 11)
margin = 5
lanes = 128


def greet(me, count):
    barrier = pltpu.get_barrier_semaphore()

    def signal(step, carry):
        pl.semaphore_signal(barrier, inc=1, device_id={"rank": lax.rem(me + step, count)})
        return carry

    lax.fori_loop(1, count, signal, 0)
    pl.semaphore_wait(barrier, count - 1)


def exchange(me, count, source_at, received, send_sem, recv_sem):
    def copy_to(step):
        peer = lax.rem(me + step, count)
        return pltpu.make_async_remote_copy(
            src_ref=source_at(peer),
            dst_ref=received.at[me],
            send_sem=send_sem.at[step],
            recv_sem=recv_sem.at[step],
            device_id={"rank": peer},
        )

    def start(step, carry):
        copy_to(step).start()
        return carry

    def wait(step, carry):
        copy_to(step).wait()
        return carry

    lax.fori_loop(1, count, start, 0)
    return lambda: lax.fori_loop(1, count, wait, 0)


def sum_kernel(count, x_ref, out_ref, received, send_sem, recv_sem):
    me = lax.axis_index("rank")
    greet(me, count)
    finish = exchange(me, count, lambda peer: x_ref.at[peer], received, send_sem, recv_sem)
    received[me] = x_ref[me]
    finish()
    out_ref[...] = received[0]

    def add(index, carry):
        out_ref[...] += received[index]
        return carry

    lax.fori_loop(1, count, add, 0)


def sum_exchange(x):
    count = x.shape[0]
    return pl.pallas_call(
        functools.partial(sum_kernel, count),
        name="sum_exchange",
        out_shape=jax.ShapeDtypeStruct(x.shape[1:], x.dtype),
        in_specs=[pl.BlockSpec(memory_space=pltpu.VMEM)],
        out_specs=pl.BlockSpec(memory_space=pltpu.VMEM),
        scratch_shapes=[
            pltpu.VMEM(x.shape, x.dtype),
            pltpu.SemaphoreType.DMA((count,)),
            pltpu.SemaphoreType.DMA((count,)),
        ],
        compiler_params=pltpu.CompilerParams(collective_id=0, has_side_effects=True),
    )(x)


def swap_kernel(count, x_ref, out_ref, send_sem, recv_sem):
    me = lax.axis_index("rank")
    greet(me, count)
    finish = exchange(me, count, lambda peer: x_ref.at[peer], out_ref, send_sem, recv_sem)
    out_ref[me] = x_ref[me]
    finish()


def swap_exchange(x):
    count = x.shape[0]
    return pl.pallas_call(
        functools.partial(swap_kernel, count),
        name="swap_exchange",
        out_shape=jax.ShapeDtypeStruct(x.shape, x.dtype),
        in_specs=[pl.BlockSpec(memory_space=pltpu.VMEM)],
        out_specs=pl.BlockSpec(memory_space=pltpu.VMEM),
        scratch_shapes=[
            pltpu.SemaphoreType.DMA((count,)),
            pltpu.SemaphoreType.DMA((count,)),
        ],
        compiler_params=pltpu.CompilerParams(collective_id=1, has_side_effects=True),
    )(x)


def stats_kernel(count, cells, x_ref, error_ref, psnr_ref, received, send_sem, recv_sem):
    me = lax.axis_index("rank")
    greet(me, count)
    finish = exchange(me, count, lambda peer: x_ref, received, send_sem, recv_sem)
    received[me] = x_ref[...]
    finish()
    largest = received[0, 0]
    total = received[0, 1]

    def add(index, carry):
        return jnp.maximum(carry[0], received[index, 0]), carry[1] + received[index, 1]

    largest, total = lax.fori_loop(1, count, add, (largest, total))
    error_ref[...] = jnp.max(largest, keepdims=True)
    mean_square = jnp.sum(total, axis=1, keepdims=True) / cells
    psnr = 10.0 * (jnp.log(peak_value * peak_value / (mean_square + epsilon)) / jnp.log(10.0))
    psnr_ref[...] = psnr


def stats_exchange(x, count, cells):
    planes = x.shape[1]
    return pl.pallas_call(
        functools.partial(stats_kernel, count, cells),
        name="stats_exchange",
        out_shape=(
            jax.ShapeDtypeStruct((1, 1), x.dtype),
            jax.ShapeDtypeStruct((planes, 1), x.dtype),
        ),
        in_specs=[pl.BlockSpec(memory_space=pltpu.VMEM)],
        out_specs=(pl.BlockSpec(memory_space=pltpu.VMEM),) * 2,
        scratch_shapes=[
            pltpu.VMEM((count,) + x.shape, x.dtype),
            pltpu.SemaphoreType.DMA((count,)),
            pltpu.SemaphoreType.DMA((count,)),
        ],
        compiler_params=pltpu.CompilerParams(collective_id=2, has_side_effects=True),
    )(x)


def shifted(pieces, shift):
    lane = lax.broadcasted_iota(jnp.int32, pieces[0].shape, 1)
    turned = [pltpu.roll(piece, lanes - shift, 1) for piece in pieces]
    inside = lane < lanes - shift
    return [
        jnp.where(inside, turned[j], turned[(j + 1) % len(turned)]) for j in range(len(turned))
    ]


def added(left, right):
    return [a + b for a, b in zip(left, right)]


def across_sums(field):
    pairs = added(field, shifted(field, 1))
    fours = added(pairs, shifted(pairs, 2))
    five = added(fours, shifted(field, 4))
    seven = added(five, shifted(pairs, 5))
    eleven = added(seven, shifted(fours, 7))
    return five, seven, eleven


def down_sums(values, window, count):
    core = values[count - 1]
    for index in range(count, window):
        core = core + values[index]
    lefts = [core]
    for index in range(count - 2, -1, -1):
        lefts.insert(0, lefts[0] + values[index])
    results = [lefts[0]]
    right = None
    for index in range(1, count):
        item = values[window + index - 1]
        right = item if right is None else right + item
        results.append(lefts[index] + right)
    return results


def similarity(a, b, q, p, window):
    area = float(window * window)
    c1 = first_const * area * area
    c2 = second_const * area * area
    ab = a * b
    mm = a * a + b * b
    upper = (ab + 0.5 * c1) * (area * p - ab + 0.5 * c2) * 4.0
    lower = (mm + c1) * (area * q - mm + c2)
    return upper / lower


def map_kernel(length, rows_step, lag, low_ref, init_ref, high_ref, rebuilt_ref,
               five_ref, seven_ref, eleven_ref, stats_ref, ext, sums, sem):
    step = pl.program_id(0)
    extended = length + 2 * margin
    ring = (lag + 1) * rows_step
    pieces = init_ref.shape[2] // lanes
    planes = init_ref.shape[1]

    @pl.when(step == 0)
    def _():
        copies = [
            pltpu.make_async_copy(low_ref, ext.at[pl.ds(0, margin)], sem.at[0]),
            pltpu.make_async_copy(init_ref, ext.at[pl.ds(margin, length)], sem.at[1]),
            pltpu.make_async_copy(high_ref, ext.at[pl.ds(margin + length, margin)], sem.at[2]),
        ]
        for copy in copies:
            copy.start()
        for copy in copies:
            copy.wait()
        stats_ref[...] = jnp.zeros_like(stats_ref)

    def one_row(index, carry):
        row = step * rows_step + index
        slot = lax.rem(row, ring)
        zero = jnp.zeros((planes, lanes), jnp.float32)
        inits = [ext[row, :, j * lanes:(j + 1) * lanes] for j in range(pieces)]
        builts = [rebuilt_ref[row, :, j * lanes:(j + 1) * lanes] for j in range(pieces)]
        own = jnp.where((row >= margin) & (row < margin + length), 1.0, 0.0)
        largest, total = zero, zero
        for a, b in zip(inits, builts):
            misfit = a - b
            largest = jnp.maximum(largest, jnp.abs(misfit))
            total = total + misfit * misfit
        stats_ref[0] = jnp.maximum(stats_ref[0], largest * own)
        stats_ref[1] += total * own
        fields = (
            inits,
            builts,
            [a * a + b * b for a, b in zip(inits, builts)],
            [a * b for a, b in zip(inits, builts)],
        )
        for number, field in enumerate(fields):
            for which, values in enumerate(across_sums(field + [zero])):
                for j, value in enumerate(values):
                    sums[slot, which * 4 + number, :, j * lanes:(j + 1) * lanes] = value
        return carry

    lax.fori_loop(0, jnp.minimum(rows_step, extended - step * rows_step), one_row, 0)

    @pl.when(step >= lag)
    def _():
        base = (step - lag) * rows_step
        lane = lax.broadcasted_iota(jnp.int32, (planes, lanes), 1)
        for which, (window, out_ref) in enumerate(zip(windows, (five_ref, seven_ref, eleven_ref))):
            half = window // 2
            first = base + margin - half
            slots = [lax.rem(first + t, ring) for t in range(rows_step + window - 1)]

            def maps_at(j, which=which, window=window, slots=slots, half=half):
                place = pl.ds(pl.multiple_of(j * lanes, lanes), lanes)
                parts = []
                for number in range(4):
                    values = [sums[slot, which * 4 + number, :, place] for slot in slots]
                    results = []
                    done = 0
                    while done < rows_step:
                        count = min(4, rows_step - done)
                        results += down_sums(values[done:done + count + window - 1], window, count)
                        done += count
                    parts.append(results)
                return tuple(
                    pltpu.roll(similarity(a, b, q, p, window), half, 1)
                    for a, b, q, p in zip(*parts)
                )

            def column(j, before, out_ref=out_ref, maps_at=maps_at, half=half):
                now = maps_at(j)
                place = pl.ds(pl.multiple_of(j * lanes, lanes), lanes)
                for index in range(rows_step):
                    out_ref[index, :, place] = jnp.where(lane < half, before[index], now[index])
                return now

            lax.fori_loop(0, pieces, column, maps_at(pieces))


def similarity_maps(low, initial, high, rebuilt):
    length, planes, across = initial.shape
    rows_step = max(size for size in range(1, 9) if length % size == 0)
    lag = -(-2 * margin // rows_step)
    out = jax.ShapeDtypeStruct(initial.shape, jnp.float32)
    out_spec = pl.BlockSpec((rows_step, planes, across), lambda s: (jnp.maximum(s - lag, 0), 0, 0))
    whole = pl.BlockSpec(memory_space=pltpu.VMEM)
    extended = length + 2 * margin
    return pl.pallas_call(
        functools.partial(map_kernel, length, rows_step, lag),
        name="similarity_maps",
        grid=(length // rows_step + lag,),
        out_shape=(out, out, out, jax.ShapeDtypeStruct((2, planes, lanes), jnp.float32)),
        in_specs=[pl.BlockSpec(memory_space=pl.ANY)] * 3 + [whole],
        out_specs=(out_spec, out_spec, out_spec, whole),
        scratch_shapes=[
            pltpu.VMEM((extended, planes, across), jnp.float32),
            pltpu.VMEM(((lag + 1) * rows_step, 12, planes, across + lanes), jnp.float32),
            pltpu.SemaphoreType.DMA((3,)),
        ],
        compiler_params=pltpu.CompilerParams(
            dimension_semantics=("arbitrary",), vmem_limit_bytes=60 * 1024 * 1024
        ),
    )(low, initial, high, rebuilt)


def body(core, x_factor, y_factor, z_factor, offsets, initial):
    exact = lax.Precision.HIGHEST
    count = lax.axis_size("rank")
    planes = offsets.shape[0]
    along, rank = x_factor.shape
    across = y_factor.shape[0]
    length = initial.shape[0]
    forward = [(i, i + 1) for i in range(count - 1)]
    backward = [(target, source) for source, target in forward]
    low = lax.ppermute(initial[length - margin:], "rank", forward)
    high = lax.ppermute(initial[:margin], "rank", backward)

    parts = count // planes
    width = rank // parts
    picked = jnp.take(z_factor, offsets, axis=1)
    partial = jnp.einsum("kab,kp->pba", core, picked, precision=exact)
    owned = sum_exchange(partial.reshape(count, width, rank))

    pack = lanes // width
    extended = length + 2 * margin
    each = -(-extended // pack)
    padded = jnp.pad(x_factor, ((margin, margin + each * pack), (0, 0)))
    blocks = jnp.stack([padded[d * length:d * length + each * pack] for d in range(count)])
    expanded = jnp.einsum("dxa,ba->dxb", blocks, owned, precision=exact)
    packed = (
        expanded.reshape(count, pack, each, width)
        .transpose(0, 2, 1, 3)
        .reshape(count, each, pack * width)
    )
    arrived = swap_exchange(packed)
    rows = (
        arrived.reshape(planes, parts, each, pack, width)
        .transpose(3, 2, 0, 1, 4)
        .reshape(pack * each, planes, rank)[:extended]
    )
    rebuilt = jnp.einsum("xpb,yb->xpy", rows, y_factor, precision=exact)
    five, seven, eleven, stats = similarity_maps(low, initial, high, rebuilt)
    error, psnr = stats_exchange(stats, count, float(along * across))
    return error.reshape(1), psnr.reshape(planes), five, seven, eleven


def solution(mesh):
    placed = (
        P("rank", "groups", None),
        P("groups", None),
        P("groups", None),
        P("rank", "groups"),
        P("groups"),
        P("rank", "groups", None),
    )
    return jax.shard_map(
        body,
        mesh=mesh,
        in_specs=placed,
        out_specs=(
            P("groups"),
            P("groups"),
            P("rank", "groups", None),
            P("rank", "groups", None),
            P("rank", "groups", None),
        ),
        check_vma=False,
    )
```

```python
import functools

import jax
import jax.numpy as jnp
from jax import lax
from jax.experimental import pallas as pl
from jax.experimental.pallas import tpu as pltpu
from jax.sharding import PartitionSpec as P

peak_value = 64.0
first_const = 0.01 * peak_value * (0.01 * peak_value)
second_const = 0.03 * peak_value * (0.03 * peak_value)
epsilon = 1e-06
windows = (5, 7, 11)
margin = 5
lanes = 128


def greet(me, count):
    barrier = pltpu.get_barrier_semaphore()

    def signal(step, carry):
        pl.semaphore_signal(barrier, inc=1, device_id={"rank": lax.rem(me + step, count)})
        return carry

    lax.fori_loop(1, count, signal, 0)
    pl.semaphore_wait(barrier, count - 1)


def exchange(me, count, source_at, received, send_sem, recv_sem):
    def copy_to(step):
        peer = lax.rem(me + step, count)
        return pltpu.make_async_remote_copy(
            src_ref=source_at(peer),
            dst_ref=received.at[me],
            send_sem=send_sem.at[step],
            recv_sem=recv_sem.at[step],
            device_id={"rank": peer},
        )

    def start(step, carry):
        copy_to(step).start()
        return carry

    def wait(step, carry):
        copy_to(step).wait()
        return carry

    lax.fori_loop(1, count, start, 0)
    return lambda: lax.fori_loop(1, count, wait, 0)


def sum_kernel(count, x_ref, out_ref, received, send_sem, recv_sem):
    me = lax.axis_index("rank")
    greet(me, count)
    finish = exchange(me, count, lambda peer: x_ref.at[peer], received, send_sem, recv_sem)
    received[me] = x_ref[me]
    finish()
    out_ref[...] = received[0]

    def add(index, carry):
        out_ref[...] += received[index]
        return carry

    lax.fori_loop(1, count, add, 0)


def sum_exchange(x):
    count = x.shape[0]
    return pl.pallas_call(
        functools.partial(sum_kernel, count),
        name="sum_exchange",
        out_shape=jax.ShapeDtypeStruct(x.shape[1:], x.dtype),
        in_specs=[pl.BlockSpec(memory_space=pltpu.VMEM)],
        out_specs=pl.BlockSpec(memory_space=pltpu.VMEM),
        scratch_shapes=[
            pltpu.VMEM(x.shape, x.dtype),
            pltpu.SemaphoreType.DMA((count,)),
            pltpu.SemaphoreType.DMA((count,)),
        ],
        compiler_params=pltpu.CompilerParams(collective_id=0, has_side_effects=True),
    )(x)


def swap_kernel(count, stride, each, x_ref, out_ref, send_sem, recv_sem):
    me = lax.axis_index("rank")

    def source_at(peer):
        return x_ref.at[pl.ds(pl.multiple_of(peer * stride, 8), each)]

    greet(me, count)
    finish = exchange(me, count, source_at, out_ref, send_sem, recv_sem)
    out_ref[me] = x_ref[pl.ds(pl.multiple_of(me * stride, 8), each)]
    finish()


def swap_exchange(x, count, stride, each):
    return pl.pallas_call(
        functools.partial(swap_kernel, count, stride, each),
        name="swap_exchange",
        out_shape=jax.ShapeDtypeStruct((count, each) + x.shape[1:], x.dtype),
        in_specs=[pl.BlockSpec(memory_space=pltpu.VMEM)],
        out_specs=pl.BlockSpec(memory_space=pltpu.VMEM),
        scratch_shapes=[
            pltpu.SemaphoreType.DMA((count,)),
            pltpu.SemaphoreType.DMA((count,)),
        ],
        compiler_params=pltpu.CompilerParams(collective_id=1, has_side_effects=True),
    )(x)


def stats_kernel(count, cells, x_ref, error_ref, psnr_ref, received, send_sem, recv_sem):
    me = lax.axis_index("rank")
    greet(me, count)
    finish = exchange(me, count, lambda peer: x_ref, received, send_sem, recv_sem)
    received[me] = x_ref[...]
    finish()
    largest = received[0, 0]
    total = received[0, 1]

    def add(index, carry):
        return jnp.maximum(carry[0], received[index, 0]), carry[1] + received[index, 1]

    largest, total = lax.fori_loop(1, count, add, (largest, total))
    error_ref[...] = jnp.max(largest, keepdims=True)
    mean_square = jnp.sum(total, axis=1, keepdims=True) / cells
    psnr = 10.0 * (jnp.log(peak_value * peak_value / (mean_square + epsilon)) / jnp.log(10.0))
    psnr_ref[...] = psnr


def stats_exchange(x, count, cells):
    planes = x.shape[1]
    return pl.pallas_call(
        functools.partial(stats_kernel, count, cells),
        name="stats_exchange",
        out_shape=(
            jax.ShapeDtypeStruct((1, 1), x.dtype),
            jax.ShapeDtypeStruct((planes, 1), x.dtype),
        ),
        in_specs=[pl.BlockSpec(memory_space=pltpu.VMEM)],
        out_specs=(pl.BlockSpec(memory_space=pltpu.VMEM),) * 2,
        scratch_shapes=[
            pltpu.VMEM((count,) + x.shape, x.dtype),
            pltpu.SemaphoreType.DMA((count,)),
            pltpu.SemaphoreType.DMA((count,)),
        ],
        compiler_params=pltpu.CompilerParams(collective_id=2, has_side_effects=True),
    )(x)


def down_sums(values, window, count):
    core = values[count - 1]
    for index in range(count, window):
        core = core + values[index]
    lefts = [core]
    for index in range(count - 2, -1, -1):
        lefts.insert(0, lefts[0] + values[index])
    results = [lefts[0]]
    right = None
    for index in range(1, count):
        item = values[window + index - 1]
        right = item if right is None else right + item
        results.append(lefts[index] + right)
    return results


def similarity(a, b, q, p, window):
    area = float(window * window)
    c1 = first_const * area * area
    c2 = second_const * area * area
    ab = a * b
    mm = a * a + b * b
    upper = (ab + 0.5 * c1) * (area * p - ab + 0.5 * c2) * 4.0
    lower = (mm + c1) * (area * q - mm + c2)
    return upper / lower


def map_kernel(length, rows_step, lag, low_ref, init_ref, high_ref, rebuilt_ref,
               five_ref, seven_ref, eleven_ref, stats_ref, ext, sums, fields, pairs, raw, sem):
    step = pl.program_id(0)
    extended = length + 2 * margin
    ring = (lag + 1) * rows_step
    pieces = init_ref.shape[2] // lanes
    planes = init_ref.shape[1]

    @pl.when(step == 0)
    def _():
        copies = [
            pltpu.make_async_copy(low_ref, ext.at[pl.ds(0, margin)], sem.at[0]),
            pltpu.make_async_copy(init_ref, ext.at[pl.ds(margin, length)], sem.at[1]),
            pltpu.make_async_copy(high_ref, ext.at[pl.ds(margin + length, margin)], sem.at[2]),
        ]
        for copy in copies:
            copy.start()
        for copy in copies:
            copy.wait()
        stats_ref[...] = jnp.zeros_like(stats_ref)

    wide = pieces * planes

    def turned(values):
        lane = lax.broadcasted_iota(jnp.int32, (8, wide), 1)
        inner = jnp.concatenate(values, axis=0).T
        rows = [inner[8 * v:8 * v + 8] for v in range(lanes // 8)]
        above = jnp.where(lane < planes, 0.0, pltpu.roll(rows[-1], planes, 1))
        below = jnp.where(lane < wide - planes, pltpu.roll(rows[0], wide - planes, 1), 0.0)
        return [above] + rows + [below]

    def one_row(index, carry):
        row = step * rows_step + index
        slot = lax.rem(row + ring - 1, ring)
        for number in range(4):
            for v in range(lanes // 8 + 2):
                pairs[number, 8 * v:8 * v + 8] = (
                    fields[number, 8 * v:8 * v + 8] + fields[number, 8 * v + 1:8 * v + 9]
                )
            for v in range(lanes // 8):
                def pair(offset, v=v, number=number):
                    return pairs[number, 8 * v + 8 + offset:8 * v + 16 + offset]

                def single(offset, v=v, number=number):
                    return fields[number, 8 * v + 8 + offset:8 * v + 16 + offset]

                five = pair(-2) + pair(0) + single(2)
                seven = five + (single(-3) + single(3))
                eleven = seven + (pair(-5) + pair(4))
                sums[slot, number, 8 * v:8 * v + 8] = five
                sums[slot, 4 + number, 8 * v:8 * v + 8] = seven
                sums[slot, 8 + number, 8 * v:8 * v + 8] = eleven
        source = jnp.minimum(row, extended - 1)
        own = jnp.where((row >= margin) & (row < margin + length), 1.0, 0.0)
        inits = [ext[source, :, j * lanes:(j + 1) * lanes] for j in range(pieces)]
        builts = [rebuilt_ref[source, :, j * lanes:(j + 1) * lanes] for j in range(pieces)]
        largest = jnp.zeros((planes, lanes), jnp.float32)
        total = largest
        for a, b in zip(inits, builts):
            misfit = a - b
            largest = jnp.maximum(largest, jnp.abs(misfit))
            total = total + misfit * misfit
        stats_ref[0] = jnp.maximum(stats_ref[0], largest * own)
        stats_ref[1] += total * own
        for v, (a, b) in enumerate(zip(turned(inits), turned(builts))):
            place = slice(8 * v, 8 * v + 8)
            fields[0, place] = a
            fields[1, place] = b
            fields[2, place] = a * a + b * b
            fields[3, place] = a * b
        return carry

    lax.fori_loop(0, jnp.minimum(rows_step, extended + 1 - step * rows_step), one_row, 0)

    @pl.when(step >= lag)
    def _():
        base = (step - lag) * rows_step
        for which, (window, out_ref) in enumerate(zip(windows, (five_ref, seven_ref, eleven_ref))):
            first = base + margin - window // 2
            slots = [lax.rem(first + t, ring) for t in range(rows_step + window - 1)]

            def maps_at(j, which=which, window=window, slots=slots):
                place = pl.ds(pl.multiple_of(j * 8, 8), 8)
                done = 0
                while done < rows_step:
                    count = min(4, rows_step - done)
                    parts = []
                    for number in range(4):
                        values = [
                            sums[slot, which * 4 + number, place]
                            for slot in slots[done:done + count + window - 1]
                        ]
                        parts.append(down_sums(values, window, count))
                    for index, (a, b, q, p) in enumerate(zip(*parts)):
                        raw[which, done + index, place] = similarity(a, b, q, p, window)
                    done += count

            def columns(pair, carry, maps_at=maps_at):
                maps_at(2 * pair)
                maps_at(2 * pair + 1)
                return carry

            lax.fori_loop(0, lanes // 16, columns, 0)
        for which, out_ref in enumerate((five_ref, seven_ref, eleven_ref)):
            for index in range(rows_step):
                back = raw[which, index].T
                for j in range(pieces):
                    out_ref[index, :, j * lanes:(j + 1) * lanes] = back[
                        j * planes:(j + 1) * planes
                    ]


def similarity_maps(low, initial, high, rebuilt):
    length, planes, across = initial.shape
    rows_step = max(size for size in range(1, 9) if length % size == 0)
    lag = -(-(2 * margin + 1) // rows_step)
    wide = planes * across // lanes
    out = jax.ShapeDtypeStruct(initial.shape, jnp.float32)
    out_spec = pl.BlockSpec((rows_step, planes, across), lambda s: (jnp.maximum(s - lag, 0), 0, 0))
    whole = pl.BlockSpec(memory_space=pltpu.VMEM)
    extended = length + 2 * margin
    return pl.pallas_call(
        functools.partial(map_kernel, length, rows_step, lag),
        name="similarity_maps",
        grid=(length // rows_step + lag,),
        out_shape=(out, out, out, jax.ShapeDtypeStruct((2, planes, lanes), jnp.float32)),
        in_specs=[pl.BlockSpec(memory_space=pl.ANY)] * 3 + [whole],
        out_specs=(out_spec, out_spec, out_spec, whole),
        scratch_shapes=[
            pltpu.VMEM((extended, planes, across), jnp.float32),
            pltpu.VMEM(((lag + 1) * rows_step, 12, lanes, wide), jnp.float32),
            pltpu.VMEM((4, lanes + 24, wide), jnp.float32),
            pltpu.VMEM((4, lanes + 24, wide), jnp.float32),
            pltpu.VMEM((3, rows_step, lanes, wide), jnp.float32),
            pltpu.SemaphoreType.DMA((3,)),
        ],
        compiler_params=pltpu.CompilerParams(
            dimension_semantics=("arbitrary",), vmem_limit_bytes=60 * 1024 * 1024
        ),
    )(low, initial, high, rebuilt)


def body(core, x_factor, y_factor, z_factor, offsets, initial):
    exact = lax.Precision.HIGHEST
    count = lax.axis_size("rank")
    planes = offsets.shape[0]
    along, rank = x_factor.shape
    across = y_factor.shape[0]
    length = initial.shape[0]
    forward = [(i, i + 1) for i in range(count - 1)]
    backward = [(target, source) for source, target in forward]
    low = lax.ppermute(initial[length - margin:], "rank", forward)
    high = lax.ppermute(initial[:margin], "rank", backward)

    parts = count // planes
    width = rank // parts
    picked = jnp.take(z_factor, offsets, axis=1)
    partial = jnp.einsum("kab,kp->pba", core, picked, precision=exact)
    owned = sum_exchange(partial.reshape(count, width, rank))

    pack = lanes // width
    extended = length + 2 * margin
    before = -(-margin // pack) * pack
    each = -(-(before - margin + extended) // (8 * pack)) * 8
    if length % (8 * pack) == 0:
        stride = length // pack
        last = (count - 1) * length + each * pack - before - along
        blocks = jnp.pad(x_factor, ((before, last), (0, 0)))
    else:
        stride = each
        padded = jnp.pad(x_factor, ((before, each * pack), (0, 0)))
        blocks = jnp.concatenate(
            [padded[d * length:d * length + each * pack] for d in range(count)]
        )
    blocks = blocks.reshape(-1, pack, rank)
    expanded = jnp.concatenate(
        [
            jnp.einsum("xa,ba->xb", blocks[:, h], owned, precision=exact)
            for h in range(pack)
        ],
        axis=1,
    )
    arrived = swap_exchange(expanded, count, stride, each)
    rows = (
        arrived.reshape(planes, parts, each, pack, width)
        .transpose(2, 3, 0, 1, 4)
        .reshape(each * pack, planes, rank)[before - margin:before - margin + extended]
    )
    rebuilt = jnp.einsum("xpb,yb->xpy", rows, y_factor, precision=exact)
    five, seven, eleven, stats = similarity_maps(low, initial, high, rebuilt)
    error, psnr = stats_exchange(stats, count, float(along * across))
    return error.reshape(1), psnr.reshape(planes), five, seven, eleven


def solution(mesh):
    placed = (
        P("rank", "groups", None),
        P("groups", None),
        P("groups", None),
        P("rank", "groups"),
        P("groups"),
        P("rank", "groups", None),
    )
    return jax.shard_map(
        body,
        mesh=mesh,
        in_specs=placed,
        out_specs=(
            P("groups"),
            P("groups"),
            P("rank", "groups", None),
            P("rank", "groups", None),
            P("rank", "groups", None),
        ),
        check_vma=False,
    )
```

```python
import functools

import jax
import jax.numpy as jnp
from jax import lax
from jax.experimental import pallas as pl
from jax.experimental.pallas import tpu as pltpu
from jax.sharding import PartitionSpec as P

peak_value = 64.0
first_const = 0.01 * peak_value * (0.01 * peak_value)
second_const = 0.03 * peak_value * (0.03 * peak_value)
epsilon = 1e-06
windows = (5, 7, 11)
margin = 5
lanes = 128


def greet(me, count):
    barrier = pltpu.get_barrier_semaphore()

    def signal(step, carry):
        pl.semaphore_signal(barrier, inc=1, device_id={"rank": lax.rem(me + step, count)})
        return carry

    lax.fori_loop(1, count, signal, 0)
    pl.semaphore_wait(barrier, count - 1)


def exchange(me, count, source_at, received, send_sem, recv_sem):
    def copy_to(step):
        peer = lax.rem(me + step, count)
        return pltpu.make_async_remote_copy(
            src_ref=source_at(peer),
            dst_ref=received.at[me],
            send_sem=send_sem.at[step],
            recv_sem=recv_sem.at[step],
            device_id={"rank": peer},
        )

    def start(step, carry):
        copy_to(step).start()
        return carry

    def wait(step, carry):
        copy_to(step).wait()
        return carry

    lax.fori_loop(1, count, start, 0)
    return lambda: lax.fori_loop(1, count, wait, 0)


def halving_orders(count, units):
    bits = [1 << j for j in range(count.bit_length() - 1)]
    rest = bits[1:]
    streams = max(1, min(3, units, len(rest)))
    return [bits[:1] + rest[k:] + rest[:k] for k in range(streams)]


def sum_kernel(count, orders, spans, x_ref, out_ref, *scratch):
    streams = len(orders)
    regions = scratch[:streams]
    send_sem, recv_sem = scratch[streams:]
    me = lax.axis_index("rank")

    def bit_of(bit):
        return lax.rem(me // bit, 2)

    def partner(bit):
        return me + bit - 2 * bit * bit_of(bit)

    barrier = pltpu.get_barrier_semaphore()
    for bit in orders[0]:
        pl.semaphore_signal(barrier, inc=1, device_id={"rank": partner(bit)})
    pl.semaphore_wait(barrier, len(orders[0]))

    def first_slot(stage):
        return count - (count >> stage)

    def held_at(stream, stage, index):
        if stage:
            return regions[stream].at[first_slot(stage - 1) + index]
        place = sum(
            lax.rem(index // (1 << j), 2) * bit for j, bit in enumerate(orders[stream])
        )
        start, size = spans[stream]
        return x_ref.at[place, pl.ds(start, size)]

    def copy_of(stream, stage, index):
        bit = orders[stream][stage]
        slot = first_slot(stage) + index
        return pltpu.make_async_remote_copy(
            src_ref=held_at(stream, stage, 1 - bit_of(bit) + 2 * index),
            dst_ref=regions[stream].at[slot],
            send_sem=send_sem.at[stream, slot],
            recv_sem=recv_sem.at[stream, slot],
            device_id={"rank": partner(bit)},
        )

    def begin(stream, stage):
        def start(index, carry):
            copy_of(stream, stage, index).start()
            return carry

        lax.fori_loop(0, count >> (stage + 1), start, 0)

    def complete(stream, stage):
        def add(index, carry):
            copy_of(stream, stage, index).wait()
            slot = first_slot(stage) + index
            mine = held_at(stream, stage, bit_of(orders[stream][stage]) + 2 * index)
            regions[stream][slot] += mine[...]
            return carry

        lax.fori_loop(0, count >> (stage + 1), add, 0)

    stages = len(orders[0])
    for stream in range(streams):
        begin(stream, 0)
    for stage in range(stages):
        for stream in range(streams):
            complete(stream, stage)
            if stage + 1 < stages:
                begin(stream, stage + 1)
    for stream, (start, size) in enumerate(spans):
        out_ref[pl.ds(start, size)] = regions[stream][count - 2]


def sum_exchange(x):
    count, rows, across = x.shape
    units = rows // 8
    orders = halving_orders(count, units)
    share = [units // len(orders) + (k < units % len(orders)) for k in range(len(orders))]
    spans = [(8 * sum(share[:k]), 8 * share[k]) for k in range(len(orders))]
    return pl.pallas_call(
        functools.partial(sum_kernel, count, orders, spans),
        name="sum_exchange",
        out_shape=jax.ShapeDtypeStruct(x.shape[1:], x.dtype),
        in_specs=[pl.BlockSpec(memory_space=pltpu.VMEM)],
        out_specs=pl.BlockSpec(memory_space=pltpu.VMEM),
        scratch_shapes=[pltpu.VMEM((count - 1, size, across), x.dtype) for _, size in spans]
        + [
            pltpu.SemaphoreType.DMA((len(orders), count - 1)),
            pltpu.SemaphoreType.DMA((len(orders), count - 1)),
        ],
        compiler_params=pltpu.CompilerParams(collective_id=0, has_side_effects=True),
    )(x)


def swap_kernel(count, stride, each, x_ref, out_ref, send_sem, recv_sem):
    me = lax.axis_index("rank")

    def source_at(peer):
        return x_ref.at[pl.ds(pl.multiple_of(peer * stride, 8), each)]

    greet(me, count)
    finish = exchange(me, count, source_at, out_ref, send_sem, recv_sem)
    out_ref[me] = x_ref[pl.ds(pl.multiple_of(me * stride, 8), each)]
    finish()


def swap_exchange(x, count, stride, each):
    return pl.pallas_call(
        functools.partial(swap_kernel, count, stride, each),
        name="swap_exchange",
        out_shape=jax.ShapeDtypeStruct((count, each) + x.shape[1:], x.dtype),
        in_specs=[pl.BlockSpec(memory_space=pltpu.VMEM)],
        out_specs=pl.BlockSpec(memory_space=pltpu.VMEM),
        scratch_shapes=[
            pltpu.SemaphoreType.DMA((count,)),
            pltpu.SemaphoreType.DMA((count,)),
        ],
        compiler_params=pltpu.CompilerParams(collective_id=1, has_side_effects=True),
    )(x)


def stats_kernel(count, cells, x_ref, error_ref, psnr_ref, received, send_sem, recv_sem):
    me = lax.axis_index("rank")
    greet(me, count)
    finish = exchange(me, count, lambda peer: x_ref, received, send_sem, recv_sem)
    received[me] = x_ref[...]
    finish()
    largest = received[0, 0]
    total = received[0, 1]

    def add(index, carry):
        return jnp.maximum(carry[0], received[index, 0]), carry[1] + received[index, 1]

    largest, total = lax.fori_loop(1, count, add, (largest, total))
    error_ref[...] = jnp.max(largest, keepdims=True)
    mean_square = jnp.sum(total, axis=1, keepdims=True) / cells
    psnr = 10.0 * (jnp.log(peak_value * peak_value / (mean_square + epsilon)) / jnp.log(10.0))
    psnr_ref[...] = psnr


def stats_exchange(x, count, cells):
    planes = x.shape[1]
    return pl.pallas_call(
        functools.partial(stats_kernel, count, cells),
        name="stats_exchange",
        out_shape=(
            jax.ShapeDtypeStruct((1, 1), x.dtype),
            jax.ShapeDtypeStruct((planes, 1), x.dtype),
        ),
        in_specs=[pl.BlockSpec(memory_space=pltpu.VMEM)],
        out_specs=(pl.BlockSpec(memory_space=pltpu.VMEM),) * 2,
        scratch_shapes=[
            pltpu.VMEM((count,) + x.shape, x.dtype),
            pltpu.SemaphoreType.DMA((count,)),
            pltpu.SemaphoreType.DMA((count,)),
        ],
        compiler_params=pltpu.CompilerParams(collective_id=2, has_side_effects=True),
    )(x)


def down_sums(values, window, count):
    core = values[count - 1]
    for index in range(count, window):
        core = core + values[index]
    lefts = [core]
    for index in range(count - 2, -1, -1):
        lefts.insert(0, lefts[0] + values[index])
    results = [lefts[0]]
    right = None
    for index in range(1, count):
        item = values[window + index - 1]
        right = item if right is None else right + item
        results.append(lefts[index] + right)
    return results


def similarity(a, b, q, p, window):
    area = float(window * window)
    c1 = first_const * area * area
    c2 = second_const * area * area
    ab = a * b
    mm = a * a + b * b
    upper = (ab + 0.5 * c1) * (area * p - ab + 0.5 * c2) * 4.0
    lower = (mm + c1) * (area * q - mm + c2)
    return upper / lower


def map_kernel(length, rows_step, lag, low_ref, init_ref, high_ref, rebuilt_ref,
               five_ref, seven_ref, eleven_ref, stats_ref, ext, sums, fields, pairs, raw, sem):
    step = pl.program_id(0)
    extended = length + 2 * margin
    ring = (lag + 1) * rows_step
    pieces = init_ref.shape[2] // lanes
    planes = init_ref.shape[1]

    @pl.when(step == 0)
    def _():
        copies = [
            pltpu.make_async_copy(low_ref, ext.at[pl.ds(0, margin)], sem.at[0]),
            pltpu.make_async_copy(init_ref, ext.at[pl.ds(margin, length)], sem.at[1]),
            pltpu.make_async_copy(high_ref, ext.at[pl.ds(margin + length, margin)], sem.at[2]),
        ]
        for copy in copies:
            copy.start()
        for copy in copies:
            copy.wait()
        stats_ref[...] = jnp.zeros_like(stats_ref)

    wide = pieces * planes

    def turned(values):
        lane = lax.broadcasted_iota(jnp.int32, (8, wide), 1)
        inner = jnp.concatenate(values, axis=0).T
        rows = [inner[8 * v:8 * v + 8] for v in range(lanes // 8)]
        above = jnp.where(lane < planes, 0.0, pltpu.roll(rows[-1], planes, 1))
        below = jnp.where(lane < wide - planes, pltpu.roll(rows[0], wide - planes, 1), 0.0)
        return [above] + rows + [below]

    def one_row(index, carry):
        row = step * rows_step + index
        slot = lax.rem(row + ring - 1, ring)
        for number in range(4):
            for v in range(lanes // 8 + 2):
                pairs[number, 8 * v:8 * v + 8] = (
                    fields[number, 8 * v:8 * v + 8] + fields[number, 8 * v + 1:8 * v + 9]
                )
            for v in range(lanes // 8):
                def pair(offset, v=v, number=number):
                    return pairs[number, 8 * v + 8 + offset:8 * v + 16 + offset]

                def single(offset, v=v, number=number):
                    return fields[number, 8 * v + 8 + offset:8 * v + 16 + offset]

                five = pair(-2) + pair(0) + single(2)
                seven = five + (single(-3) + single(3))
                eleven = seven + (pair(-5) + pair(4))
                sums[slot, number, 8 * v:8 * v + 8] = five
                sums[slot, 4 + number, 8 * v:8 * v + 8] = seven
                sums[slot, 8 + number, 8 * v:8 * v + 8] = eleven
        source = jnp.minimum(row, extended - 1)
        own = jnp.where((row >= margin) & (row < margin + length), 1.0, 0.0)
        inits = [ext[source, :, j * lanes:(j + 1) * lanes] for j in range(pieces)]
        builts = [rebuilt_ref[source, :, j * lanes:(j + 1) * lanes] for j in range(pieces)]
        largest = jnp.zeros((planes, lanes), jnp.float32)
        total = largest
        for a, b in zip(inits, builts):
            misfit = a - b
            largest = jnp.maximum(largest, jnp.abs(misfit))
            total = total + misfit * misfit
        stats_ref[0] = jnp.maximum(stats_ref[0], largest * own)
        stats_ref[1] += total * own
        for v, (a, b) in enumerate(zip(turned(inits), turned(builts))):
            place = slice(8 * v, 8 * v + 8)
            fields[0, place] = a
            fields[1, place] = b
            fields[2, place] = a * a + b * b
            fields[3, place] = a * b
        return carry

    lax.fori_loop(0, jnp.minimum(rows_step, extended + 1 - step * rows_step), one_row, 0)

    @pl.when(step >= lag)
    def _():
        base = (step - lag) * rows_step
        for which, (window, out_ref) in enumerate(zip(windows, (five_ref, seven_ref, eleven_ref))):
            first = base + margin - window // 2
            slots = [lax.rem(first + t, ring) for t in range(rows_step + window - 1)]

            def maps_at(j, which=which, window=window, slots=slots):
                place = pl.ds(pl.multiple_of(j * 8, 8), 8)
                done = 0
                while done < rows_step:
                    count = min(4, rows_step - done)
                    parts = []
                    for number in range(4):
                        values = [
                            sums[slot, which * 4 + number, place]
                            for slot in slots[done:done + count + window - 1]
                        ]
                        parts.append(down_sums(values, window, count))
                    for index, (a, b, q, p) in enumerate(zip(*parts)):
                        raw[which, done + index, place] = similarity(a, b, q, p, window)
                    done += count

            def columns(pair, carry, maps_at=maps_at):
                maps_at(2 * pair)
                maps_at(2 * pair + 1)
                return carry

            lax.fori_loop(0, lanes // 16, columns, 0)
        for which, out_ref in enumerate((five_ref, seven_ref, eleven_ref)):
            for index in range(rows_step):
                back = raw[which, index].T
                for j in range(pieces):
                    out_ref[index, :, j * lanes:(j + 1) * lanes] = back[
                        j * planes:(j + 1) * planes
                    ]


def similarity_maps(low, initial, high, rebuilt):
    length, planes, across = initial.shape
    rows_step = max(size for size in range(1, 9) if length % size == 0)
    lag = -(-(2 * margin + 1) // rows_step)
    wide = planes * across // lanes
    out = jax.ShapeDtypeStruct(initial.shape, jnp.float32)
    out_spec = pl.BlockSpec((rows_step, planes, across), lambda s: (jnp.maximum(s - lag, 0), 0, 0))
    whole = pl.BlockSpec(memory_space=pltpu.VMEM)
    extended = length + 2 * margin
    return pl.pallas_call(
        functools.partial(map_kernel, length, rows_step, lag),
        name="similarity_maps",
        grid=(length // rows_step + lag,),
        out_shape=(out, out, out, jax.ShapeDtypeStruct((2, planes, lanes), jnp.float32)),
        in_specs=[pl.BlockSpec(memory_space=pl.ANY)] * 3 + [whole],
        out_specs=(out_spec, out_spec, out_spec, whole),
        scratch_shapes=[
            pltpu.VMEM((extended, planes, across), jnp.float32),
            pltpu.VMEM(((lag + 1) * rows_step, 12, lanes, wide), jnp.float32),
            pltpu.VMEM((4, lanes + 24, wide), jnp.float32),
            pltpu.VMEM((4, lanes + 24, wide), jnp.float32),
            pltpu.VMEM((3, rows_step, lanes, wide), jnp.float32),
            pltpu.SemaphoreType.DMA((3,)),
        ],
        compiler_params=pltpu.CompilerParams(
            dimension_semantics=("arbitrary",), vmem_limit_bytes=60 * 1024 * 1024
        ),
    )(low, initial, high, rebuilt)


def body(core, x_factor, y_factor, z_factor, offsets, initial):
    exact = lax.Precision.HIGHEST
    count = lax.axis_size("rank")
    planes = offsets.shape[0]
    along, rank = x_factor.shape
    across = y_factor.shape[0]
    length = initial.shape[0]
    forward = [(i, i + 1) for i in range(count - 1)]
    backward = [(target, source) for source, target in forward]
    low = lax.ppermute(initial[length - margin:], "rank", forward)
    high = lax.ppermute(initial[:margin], "rank", backward)

    parts = count // planes
    width = rank // parts
    picked = jnp.take(z_factor, offsets, axis=1)
    partial = jnp.einsum("kab,kp->pba", core, picked, precision=exact)
    owned = sum_exchange(partial.reshape(count, width, rank))

    pack = lanes // width
    extended = length + 2 * margin
    each = -(-extended // (8 * pack)) * 8
    expanded = jnp.einsum("xa,ba->xb", x_factor, owned, precision=exact)
    total = (count - 1) * length + each
    padded = jnp.pad(expanded, ((margin, pack * each), (0, 0)))
    expanded = jnp.concatenate(
        [padded[h * each:h * each + total] for h in range(pack)], axis=1
    )
    stride = length
    if length % 8:
        stride = each
        expanded = jnp.concatenate(
            [expanded[d * length:d * length + each] for d in range(count)]
        )
    arrived = swap_exchange(expanded, count, stride, each)
    rows = (
        arrived.reshape(planes, parts, each, pack, width)
        .transpose(3, 2, 0, 1, 4)
        .reshape(each * pack, planes, rank)[:extended]
    )
    rebuilt = jnp.einsum("xpb,yb->xpy", rows, y_factor, precision=exact)
    five, seven, eleven, stats = similarity_maps(low, initial, high, rebuilt)
    error, psnr = stats_exchange(stats, count, float(along * across))
    return error.reshape(1), psnr.reshape(planes), five, seven, eleven


def solution(mesh):
    placed = (
        P("rank", "groups", None),
        P("groups", None),
        P("groups", None),
        P("rank", "groups"),
        P("groups"),
        P("rank", "groups", None),
    )
    return jax.shard_map(
        body,
        mesh=mesh,
        in_specs=placed,
        out_specs=(
            P("groups"),
            P("groups"),
            P("rank", "groups", None),
            P("rank", "groups", None),
            P("rank", "groups", None),
        ),
        check_vma=False,
    )
```

```python
import functools

import jax
import jax.numpy as jnp
from jax import lax
from jax.experimental import pallas as pl
from jax.experimental.pallas import tpu as pltpu
from jax.sharding import PartitionSpec as P

peak_value = 64.0
first_const = 0.01 * peak_value * (0.01 * peak_value)
second_const = 0.03 * peak_value * (0.03 * peak_value)
epsilon = 1e-06
windows = (5, 7, 11)
margin = 5
lanes = 128


def greet(me, count):
    barrier = pltpu.get_barrier_semaphore()

    def signal(step, carry):
        pl.semaphore_signal(barrier, inc=1, device_id={"rank": lax.rem(me + step, count)})
        return carry

    lax.fori_loop(1, count, signal, 0)
    pl.semaphore_wait(barrier, count - 1)


def exchange(me, count, source_at, received, send_sem, recv_sem):
    def copy_to(step):
        peer = lax.rem(me + step, count)
        return pltpu.make_async_remote_copy(
            src_ref=source_at(peer),
            dst_ref=received.at[me],
            send_sem=send_sem.at[step],
            recv_sem=recv_sem.at[step],
            device_id={"rank": peer},
        )

    def start(step, carry):
        copy_to(step).start()
        return carry

    def wait(step, carry):
        copy_to(step).wait()
        return carry

    lax.fori_loop(1, count, start, 0)
    return lambda: lax.fori_loop(1, count, wait, 0)


def halving_orders(count, units):
    bits = [1 << j for j in range(count.bit_length() - 1)]
    rest = bits[1:]
    streams = max(1, min(3, units, len(rest)))
    return [bits[:1] + rest[k:] + rest[:k] for k in range(streams)]


def sum_kernel(count, orders, spans, x_ref, out_ref, *scratch):
    streams = len(orders)
    regions = scratch[:streams]
    send_sem, recv_sem = scratch[streams:]
    me = lax.axis_index("rank")

    def bit_of(bit):
        return lax.rem(me // bit, 2)

    def partner(bit):
        return me + bit - 2 * bit * bit_of(bit)

    barrier = pltpu.get_barrier_semaphore()
    for bit in orders[0]:
        pl.semaphore_signal(barrier, inc=1, device_id={"rank": partner(bit)})
    pl.semaphore_wait(barrier, len(orders[0]))

    def first_slot(stage):
        return count - (count >> stage)

    def held_at(stream, stage, index):
        if stage:
            return regions[stream].at[first_slot(stage - 1) + index]
        place = sum(
            lax.rem(index // (1 << j), 2) * bit for j, bit in enumerate(orders[stream])
        )
        start, size = spans[stream]
        return x_ref.at[place, pl.ds(start, size)]

    def copy_of(stream, stage, index):
        bit = orders[stream][stage]
        slot = first_slot(stage) + index
        return pltpu.make_async_remote_copy(
            src_ref=held_at(stream, stage, 1 - bit_of(bit) + 2 * index),
            dst_ref=regions[stream].at[slot],
            send_sem=send_sem.at[stream, slot],
            recv_sem=recv_sem.at[stream, slot],
            device_id={"rank": partner(bit)},
        )

    def begin(stream, stage):
        def start(index, carry):
            copy_of(stream, stage, index).start()
            return carry

        lax.fori_loop(0, count >> (stage + 1), start, 0)

    def complete(stream, stage):
        def add(index, carry):
            copy_of(stream, stage, index).wait()
            slot = first_slot(stage) + index
            mine = held_at(stream, stage, bit_of(orders[stream][stage]) + 2 * index)
            regions[stream][slot] += mine[...]
            return carry

        lax.fori_loop(0, count >> (stage + 1), add, 0)

    stages = len(orders[0])
    for stream in range(streams):
        begin(stream, 0)
    for stage in range(stages):
        for stream in range(streams):
            complete(stream, stage)
            if stage + 1 < stages:
                begin(stream, stage + 1)
    for stream, (start, size) in enumerate(spans):
        out_ref[pl.ds(start, size)] = regions[stream][count - 2]


def sum_exchange(x):
    count, rows, across = x.shape
    units = rows // 8
    orders = halving_orders(count, units)
    share = [units // len(orders) + (k < units % len(orders)) for k in range(len(orders))]
    spans = [(8 * sum(share[:k]), 8 * share[k]) for k in range(len(orders))]
    return pl.pallas_call(
        functools.partial(sum_kernel, count, orders, spans),
        name="sum_exchange",
        out_shape=jax.ShapeDtypeStruct(x.shape[1:], x.dtype),
        in_specs=[pl.BlockSpec(memory_space=pltpu.VMEM)],
        out_specs=pl.BlockSpec(memory_space=pltpu.VMEM),
        scratch_shapes=[pltpu.VMEM((count - 1, size, across), x.dtype) for _, size in spans]
        + [
            pltpu.SemaphoreType.DMA((len(orders), count - 1)),
            pltpu.SemaphoreType.DMA((len(orders), count - 1)),
        ],
        compiler_params=pltpu.CompilerParams(collective_id=0, has_side_effects=True),
    )(x)


def swap_kernel(count, stride, each, x_ref, out_ref, send_sem, recv_sem):
    me = lax.axis_index("rank")

    def source_at(peer):
        return x_ref.at[pl.ds(pl.multiple_of(peer * stride, 8), each)]

    greet(me, count)
    finish = exchange(me, count, source_at, out_ref, send_sem, recv_sem)
    out_ref[me] = x_ref[pl.ds(pl.multiple_of(me * stride, 8), each)]
    finish()


def swap_exchange(x, count, stride, each):
    return pl.pallas_call(
        functools.partial(swap_kernel, count, stride, each),
        name="swap_exchange",
        out_shape=jax.ShapeDtypeStruct((count, each) + x.shape[1:], x.dtype),
        in_specs=[pl.BlockSpec(memory_space=pltpu.VMEM)],
        out_specs=pl.BlockSpec(memory_space=pltpu.VMEM),
        scratch_shapes=[
            pltpu.SemaphoreType.DMA((count,)),
            pltpu.SemaphoreType.DMA((count,)),
        ],
        compiler_params=pltpu.CompilerParams(collective_id=1, has_side_effects=True),
    )(x)


def stats_kernel(count, cells, x_ref, error_ref, psnr_ref, held, received, send_sem, recv_sem):
    me = lax.axis_index("rank")
    bits = [1 << j for j in range(count.bit_length() - 1)]
    partners = [me + bit - 2 * bit * lax.rem(me // bit, 2) for bit in bits]
    barrier = pltpu.get_barrier_semaphore()
    for partner in partners:
        pl.semaphore_signal(barrier, inc=1, device_id={"rank": partner})
    pl.semaphore_wait(barrier, len(bits))
    held[0] = x_ref[...]
    for stage, partner in enumerate(partners):
        copy = pltpu.make_async_remote_copy(
            src_ref=held.at[stage],
            dst_ref=received.at[stage],
            send_sem=send_sem.at[stage],
            recv_sem=recv_sem.at[stage],
            device_id={"rank": partner},
        )
        copy.start()
        copy.wait()
        held[stage + 1, 0] = jnp.maximum(held[stage, 0], received[stage, 0])
        held[stage + 1, 1] = held[stage, 1] + received[stage, 1]
    error_ref[...] = jnp.max(held[len(bits), 0], keepdims=True)
    mean_square = jnp.sum(held[len(bits), 1], axis=1, keepdims=True) / cells
    psnr = 10.0 * (jnp.log(peak_value * peak_value / (mean_square + epsilon)) / jnp.log(10.0))
    psnr_ref[...] = psnr


def stats_exchange(x, count, cells):
    planes = x.shape[1]
    return pl.pallas_call(
        functools.partial(stats_kernel, count, cells),
        name="stats_exchange",
        out_shape=(
            jax.ShapeDtypeStruct((1, 1), x.dtype),
            jax.ShapeDtypeStruct((planes, 1), x.dtype),
        ),
        in_specs=[pl.BlockSpec(memory_space=pltpu.VMEM)],
        out_specs=(pl.BlockSpec(memory_space=pltpu.VMEM),) * 2,
        scratch_shapes=[
            pltpu.VMEM((count.bit_length(),) + x.shape, x.dtype),
            pltpu.VMEM((count.bit_length(),) + x.shape, x.dtype),
            pltpu.SemaphoreType.DMA((count.bit_length(),)),
            pltpu.SemaphoreType.DMA((count.bit_length(),)),
        ],
        compiler_params=pltpu.CompilerParams(collective_id=2, has_side_effects=True),
    )(x)


def down_sums(values, window, count):
    core = values[count - 1]
    for index in range(count, window):
        core = core + values[index]
    lefts = [core]
    for index in range(count - 2, -1, -1):
        lefts.insert(0, lefts[0] + values[index])
    results = [lefts[0]]
    right = None
    for index in range(1, count):
        item = values[window + index - 1]
        right = item if right is None else right + item
        results.append(lefts[index] + right)
    return results


def similarity(a, b, q, p, window):
    area = float(window * window)
    c1 = first_const * area * area
    c2 = second_const * area * area
    ab = a * b
    mm = a * a + b * b
    upper = (ab + 0.5 * c1) * (area * p - ab + 0.5 * c2) * 4.0
    lower = (mm + c1) * (area * q - mm + c2)
    return upper / lower


def map_kernel(length, rows_step, lag, low_ref, init_ref, high_ref, rebuilt_ref,
               five_ref, seven_ref, eleven_ref, stats_ref, ext, sums, fields, pairs, raw, sem):
    step = pl.program_id(0)
    extended = length + 2 * margin
    ring = (lag + 1) * rows_step
    pieces = init_ref.shape[2] // lanes
    planes = init_ref.shape[1]

    @pl.when(step == 0)
    def _():
        copies = [
            pltpu.make_async_copy(low_ref, ext.at[pl.ds(0, margin)], sem.at[0]),
            pltpu.make_async_copy(init_ref, ext.at[pl.ds(margin, length)], sem.at[1]),
            pltpu.make_async_copy(high_ref, ext.at[pl.ds(margin + length, margin)], sem.at[2]),
        ]
        for copy in copies:
            copy.start()
        for copy in copies:
            copy.wait()
        stats_ref[...] = jnp.zeros_like(stats_ref)

    wide = pieces * planes

    def turned(values):
        lane = lax.broadcasted_iota(jnp.int32, (8, wide), 1)
        inner = jnp.concatenate(values, axis=0).T
        rows = [inner[8 * v:8 * v + 8] for v in range(lanes // 8)]
        above = jnp.where(lane < planes, 0.0, pltpu.roll(rows[-1], planes, 1))
        below = jnp.where(lane < wide - planes, pltpu.roll(rows[0], wide - planes, 1), 0.0)
        return [above] + rows + [below]

    def one_row(index, carry):
        row = step * rows_step + index
        slot = lax.rem(row + ring - 1, ring)
        for number in range(4):
            for v in range(lanes // 8 + 2):
                pairs[number, 8 * v:8 * v + 8] = (
                    fields[number, 8 * v:8 * v + 8] + fields[number, 8 * v + 1:8 * v + 9]
                )
            for v in range(lanes // 8):
                def pair(offset, v=v, number=number):
                    return pairs[number, 8 * v + 8 + offset:8 * v + 16 + offset]

                def single(offset, v=v, number=number):
                    return fields[number, 8 * v + 8 + offset:8 * v + 16 + offset]

                five = pair(-2) + pair(0) + single(2)
                seven = five + (single(-3) + single(3))
                eleven = seven + (pair(-5) + pair(4))
                sums[slot, number, 8 * v:8 * v + 8] = five
                sums[slot, 4 + number, 8 * v:8 * v + 8] = seven
                sums[slot, 8 + number, 8 * v:8 * v + 8] = eleven
        source = jnp.minimum(row, extended - 1)
        own = jnp.where((row >= margin) & (row < margin + length), 1.0, 0.0)
        inits = [ext[source, :, j * lanes:(j + 1) * lanes] for j in range(pieces)]
        builts = [rebuilt_ref[source, :, j * lanes:(j + 1) * lanes] for j in range(pieces)]
        largest = jnp.zeros((planes, lanes), jnp.float32)
        total = largest
        for a, b in zip(inits, builts):
            misfit = a - b
            largest = jnp.maximum(largest, jnp.abs(misfit))
            total = total + misfit * misfit
        stats_ref[0] = jnp.maximum(stats_ref[0], largest * own)
        stats_ref[1] += total * own
        for v, (a, b) in enumerate(zip(turned(inits), turned(builts))):
            place = slice(8 * v, 8 * v + 8)
            fields[0, place] = a
            fields[1, place] = b
            fields[2, place] = a * a + b * b
            fields[3, place] = a * b
        return carry

    lax.fori_loop(0, jnp.minimum(rows_step, extended + 1 - step * rows_step), one_row, 0)

    @pl.when(step >= lag)
    def _():
        base = (step - lag) * rows_step
        for which, (window, out_ref) in enumerate(zip(windows, (five_ref, seven_ref, eleven_ref))):
            first = base + margin - window // 2
            slots = [lax.rem(first + t, ring) for t in range(rows_step + window - 1)]

            def maps_at(j, which=which, window=window, slots=slots):
                place = pl.ds(pl.multiple_of(j * 8, 8), 8)
                done = 0
                while done < rows_step:
                    count = min(4, rows_step - done)
                    parts = []
                    for number in range(4):
                        values = [
                            sums[slot, which * 4 + number, place]
                            for slot in slots[done:done + count + window - 1]
                        ]
                        parts.append(down_sums(values, window, count))
                    for index, (a, b, q, p) in enumerate(zip(*parts)):
                        raw[which, done + index, place] = similarity(a, b, q, p, window)
                    done += count

            def columns(pair, carry, maps_at=maps_at):
                maps_at(2 * pair)
                maps_at(2 * pair + 1)
                return carry

            lax.fori_loop(0, lanes // 16, columns, 0)
        for which, out_ref in enumerate((five_ref, seven_ref, eleven_ref)):
            for index in range(rows_step):
                back = raw[which, index].T
                for j in range(pieces):
                    out_ref[index, :, j * lanes:(j + 1) * lanes] = back[
                        j * planes:(j + 1) * planes
                    ]


def similarity_maps(low, initial, high, rebuilt):
    length, planes, across = initial.shape
    rows_step = max(size for size in range(1, 9) if length % size == 0)
    lag = -(-(2 * margin + 1) // rows_step)
    wide = planes * across // lanes
    out = jax.ShapeDtypeStruct(initial.shape, jnp.float32)
    out_spec = pl.BlockSpec((rows_step, planes, across), lambda s: (jnp.maximum(s - lag, 0), 0, 0))
    whole = pl.BlockSpec(memory_space=pltpu.VMEM)
    extended = length + 2 * margin
    return pl.pallas_call(
        functools.partial(map_kernel, length, rows_step, lag),
        name="similarity_maps",
        grid=(length // rows_step + lag,),
        out_shape=(out, out, out, jax.ShapeDtypeStruct((2, planes, lanes), jnp.float32)),
        in_specs=[pl.BlockSpec(memory_space=pl.ANY)] * 3 + [whole],
        out_specs=(out_spec, out_spec, out_spec, whole),
        scratch_shapes=[
            pltpu.VMEM((extended, planes, across), jnp.float32),
            pltpu.VMEM(((lag + 1) * rows_step, 12, lanes, wide), jnp.float32),
            pltpu.VMEM((4, lanes + 24, wide), jnp.float32),
            pltpu.VMEM((4, lanes + 24, wide), jnp.float32),
            pltpu.VMEM((3, rows_step, lanes, wide), jnp.float32),
            pltpu.SemaphoreType.DMA((3,)),
        ],
        compiler_params=pltpu.CompilerParams(
            dimension_semantics=("arbitrary",), vmem_limit_bytes=60 * 1024 * 1024
        ),
    )(low, initial, high, rebuilt)


def body(core, x_factor, y_factor, z_factor, offsets, initial):
    exact = lax.Precision.HIGHEST
    count = lax.axis_size("rank")
    planes = offsets.shape[0]
    along, rank = x_factor.shape
    across = y_factor.shape[0]
    length = initial.shape[0]
    forward = [(i, i + 1) for i in range(count - 1)]
    backward = [(target, source) for source, target in forward]
    low = lax.ppermute(initial[length - margin:], "rank", forward)
    high = lax.ppermute(initial[:margin], "rank", backward)

    parts = count // planes
    width = rank // parts
    picked = jnp.take(z_factor, offsets, axis=1)
    partial = jnp.einsum("kab,kp->pba", core, picked, precision=exact)
    owned = sum_exchange(partial.reshape(count, width, rank))

    pack = lanes // width
    extended = length + 2 * margin
    each = -(-extended // (8 * pack)) * 8
    expanded = jnp.einsum("xa,ba->xb", x_factor, owned, precision=exact)
    total = (count - 1) * length + each
    padded = jnp.pad(expanded, ((margin, pack * each), (0, 0)))
    expanded = jnp.concatenate(
        [padded[h * each:h * each + total] for h in range(pack)], axis=1
    )
    stride = length
    if length % 8:
        stride = each
        expanded = jnp.concatenate(
            [expanded[d * length:d * length + each] for d in range(count)]
        )
    arrived = swap_exchange(expanded, count, stride, each)
    rows = (
        arrived.reshape(planes, parts, each, pack, width)
        .transpose(3, 2, 0, 1, 4)
        .reshape(each * pack, planes, rank)[:extended]
    )
    rebuilt = jnp.einsum("xpb,yb->xpy", rows, y_factor, precision=exact)
    five, seven, eleven, stats = similarity_maps(low, initial, high, rebuilt)
    error, psnr = stats_exchange(stats, count, float(along * across))
    return error.reshape(1), psnr.reshape(planes), five, seven, eleven


def solution(mesh):
    placed = (
        P("rank", "groups", None),
        P("groups", None),
        P("groups", None),
        P("rank", "groups"),
        P("groups"),
        P("rank", "groups", None),
    )
    return jax.shard_map(
        body,
        mesh=mesh,
        in_specs=placed,
        out_specs=(
            P("groups"),
            P("groups"),
            P("rank", "groups", None),
            P("rank", "groups", None),
            P("rank", "groups", None),
        ),
        check_vma=False,
    )
```
